32 devices in a mesh: vol: 16 (over z, x, core), slab: 2 (over y).
Axes of the slice: x: 2, y: 2, z: 4, core: 2. Of those that a mesh axis runs over, the one named last changes fastest.
Arguments:
- volumes: bfloat16 [32, 4, 16, 16, 64], P('vol', None, 'slab'), may hold values from -6 to 6
- w_first: bfloat16 [32, 108], replicated, may hold values from -0.625 to 0.625
- w_second: bfloat16 [64, 864], replicated, may hold values from -0.21875 to 0.21875
- w_third: bfloat16 [128, 1728], replicated, may hold values from -0.15625 to 0.15625
- map_grad: bfloat16 [32, 128, 4, 4, 16], P(('vol', 'slab')), may hold values from -6 to 6
Outputs:
- grad_first: float32 [32, 108], replicated
- grad_second: float32 [64, 864], replicated
- grad_third: float32 [128, 1728], replicated
The draws below stay inside these ranges and needn't reach their ends.
All inputs are finite; a program needn't handle non-finite values.
Results may differ from the reference program's by a relative error of at most 0.0071.
Values may be sent and summed in bfloat16 or wider, within the bound.
A program may use at most 64 MiB of HBM per device.

```python
import jax
import jax.numpy as jnp
from jax import lax

C0 = 4
C1 = 32
C2 = 64
C3 = 128
VX = 64
VY = 16
VZ = 16
SAMPLES = 32


def shard_levels(rng, shape, cuts, smallest, top_value):
    loudness = 1.0
    for axis_at, blocks in cuts:
        heights = jax.random.uniform(jax.random.fold_in(jax.random.fold_in(rng, 6), axis_at), (blocks,), jnp.float32, smallest / len(cuts), top_value / len(cuts))
        loudness = loudness * jnp.repeat(jnp.exp(heights), shape[axis_at] // blocks).reshape((-1,) + (1,) * (len(shape) - 1 - axis_at))
    return loudness


def noise(key, dims, width, most, split=(), kind=jnp.bfloat16):
    loudness = shard_levels(key, dims, split, -0.22, 0.18) if split else 1.0
    array = jax.random.normal(key, dims, jnp.float32) * width * loudness
    return jnp.minimum(jnp.maximum(array, -most), most).astype(kind)


def setup_inputs(seed: int = 0) -> dict:
    splits = jax.random.split(jax.random.key(seed), 6)
    volumes = noise(splits[0], (SAMPLES, C0, VZ, VY, VX), 1.0, 6.0, ((0, 16), (2, 2)))
    w_first = noise(splits[1], (C1, 27 * C0), (27 * C0) ** -0.5, 0.625)
    w_second = noise(splits[2], (C2, 27 * C1), (27 * C1) ** -0.5, 0.21875)
    w_third = noise(splits[3], (C3, 27 * C2), (27 * C2) ** -0.5, 0.15625)
    map_grad = noise(splits[4], (SAMPLES, C3, VZ // 4, VY // 4, VX // 4), 1.0, 6.0, ((0, 32),))
    return {"volumes": volumes, "w_first": w_first, "w_second": w_second, "w_third": w_third, "map_grad": map_grad}


FORWARD_DIMS = ('NCDHW', 'OIDHW', 'NCDHW')
FILTER_DIMS = ('CNDHW', 'IODHW', 'CNDHW')
SPREAD_DIMS = ('NCDHW', 'IODHW', 'NCDHW')

def kernel_of(weight):
    channels = weight.shape[1] // 27
    return weight.reshape(weight.shape[0], 3, 3, 3, channels).transpose(0, 4, 1, 2, 3)

def flat_of(kernel):
    return kernel.transpose(0, 2, 3, 4, 1).reshape(kernel.shape[0], -1)

def forward(maps, weight, stride, pads):
    return lax.conv_general_dilated(maps.astype(jnp.float32), kernel_of(weight).astype(jnp.float32), (stride, stride, stride), pads, dimension_numbers=FORWARD_DIMS, precision=lax.Precision.HIGHEST)

def weight_grad(maps, delta, stride, pads):
    bounds = []
    for dim_index in range(3):
        extent = maps.shape[2 + dim_index]
        lower = pads[dim_index][0]
        cells_out = delta.shape[2 + dim_index]
        bounds.append((lower, 3 - extent - lower + (cells_out - 1) * stride))
    kernel = lax.conv_general_dilated(maps.astype(jnp.float32), delta.astype(jnp.float32), (1, 1, 1), bounds, rhs_dilation=(stride, stride, stride), dimension_numbers=FILTER_DIMS, precision=lax.Precision.HIGHEST)
    return flat_of(kernel)

def spread_back(delta, weight, stride):
    kernel = kernel_of(weight)[:, :, ::-1, ::-1, ::-1].astype(jnp.float32)
    return lax.conv_general_dilated(delta.astype(jnp.float32), kernel, (1, 1, 1), ((2, 2), (2, 2), (2, 2)), lhs_dilation=(stride, stride, stride), dimension_numbers=SPREAD_DIMS, precision=lax.Precision.HIGHEST)

def interior(full, shape):
    return full[:, :, 1:1 + shape[2], 1:1 + shape[3], 1:1 + shape[4]]

def silu_slope(pre):
    sigma = jax.nn.sigmoid(pre)
    return sigma * (1.0 + pre * (1.0 - sigma))

def reference(volumes, w_first, w_second, w_third, map_grad):
    full_pads = ((1, 1), (1, 1), (1, 1))

    def one_sample(totals, inputs):
        volume, grad_map = inputs
        volume = volume[None]
        pre_first = forward(volume, w_first, 2, full_pads)
        act_first = jax.nn.silu(pre_first).astype(jnp.bfloat16)
        pre_second = forward(act_first, w_second, 2, full_pads)
        act_second = jax.nn.silu(pre_second).astype(jnp.bfloat16)
        pre_third = forward(act_second, w_third, 1, full_pads)
        delta_third = (grad_map[None].astype(jnp.float32) * silu_slope(pre_third)).astype(jnp.bfloat16)
        step_third = weight_grad(act_second, delta_third, 1, full_pads)
        back_second = interior(spread_back(delta_third, w_third, 1), act_second.shape).astype(jnp.bfloat16)
        delta_second = (back_second.astype(jnp.float32) * silu_slope(pre_second)).astype(jnp.bfloat16)
        step_second = weight_grad(act_first, delta_second, 2, full_pads)
        back_first = interior(spread_back(delta_second, w_second, 2), act_first.shape)
        delta_first = (back_first * silu_slope(pre_first)).astype(jnp.bfloat16)
        step_first = weight_grad(volume, delta_first, 2, full_pads)
        return ((totals[0] + step_first, totals[1] + step_second, totals[2] + step_third), None)
    start = (jnp.zeros((C1, 27 * C0), jnp.float32), jnp.zeros((C2, 27 * C1), jnp.float32), jnp.zeros((C3, 27 * C2), jnp.float32))
    totals, unused = lax.scan(one_sample, start, (volumes, map_grad))
    factor = 1.0 / SAMPLES
    return (totals[0] * factor, totals[1] * factor, totals[2] * factor)
```

```python
import functools

import jax
import jax.numpy as jnp
from jax import lax
from jax.experimental import pallas as pl
from jax.experimental.pallas import tpu as pltpu
from jax.sharding import PartitionSpec as P

MESH = pl.DeviceIdType.MESH
FORWARD_DIMS = ("NCDHW", "OIDHW", "NCDHW")
FILTER_DIMS = ("CNDHW", "IODHW", "CNDHW")
SPREAD_DIMS = ("NCDHW", "IODHW", "NCDHW")


def shifted(array, axis, by):
    length = lax.axis_size(axis)
    pairs = [(i, i + by) for i in range(length) if 0 <= i + by < length]
    return lax.ppermute(array, axis, pairs)


def kernel_of(weight):
    channels = weight.shape[1] // 27
    return weight.reshape(weight.shape[0], 3, 3, 3, channels).transpose(0, 4, 1, 2, 3)


def flat_of(kernel):
    return kernel.transpose(0, 2, 3, 4, 1).reshape(kernel.shape[0], -1)


def forward(maps, weight, stride, pads):
    return lax.conv_general_dilated(
        maps,
        kernel_of(weight),
        (stride, stride, stride),
        pads,
        dimension_numbers=FORWARD_DIMS,
        preferred_element_type=jnp.float32,
    )


def weight_grad(maps, delta, stride, pads):
    bounds = []
    for dim_index in range(3):
        extent = maps.shape[2 + dim_index]
        lower = pads[dim_index][0]
        cells_out = delta.shape[2 + dim_index]
        bounds.append((lower, 3 - extent - lower + (cells_out - 1) * stride))
    kernel = lax.conv_general_dilated(
        maps,
        delta,
        (1, 1, 1),
        bounds,
        rhs_dilation=(stride, stride, stride),
        dimension_numbers=FILTER_DIMS,
        preferred_element_type=jnp.float32,
    )
    return flat_of(kernel)


def spread_back(delta, weight, stride):
    kernel = kernel_of(weight)[:, :, ::-1, ::-1, ::-1]
    return lax.conv_general_dilated(
        delta,
        kernel,
        (1, 1, 1),
        ((2, 2), (2, 2), (2, 2)),
        lhs_dilation=(stride, stride, stride),
        dimension_numbers=SPREAD_DIMS,
        preferred_element_type=jnp.float32,
    )


def interior(full, shape):
    return full[:, :, 1 : 1 + shape[2], 1 : 1 + shape[3], 1 : 1 + shape[4]]


def silu_slope(pre):
    sigma = jax.nn.sigmoid(pre)
    return sigma * (1.0 + pre * (1.0 - sigma))


def packed_rows(shapes):
    return sum(pl.cdiv(cols, 128) * rows for rows, cols in shapes)


def tiles_of(shapes):
    base = 0
    for index, (rows, cols) in enumerate(shapes):
        for start in range(0, cols, 128):
            yield index, base, rows, start, min(128, cols - start)
            base += rows


def piece_rows(shapes, devices):
    return pl.cdiv(pl.cdiv(packed_rows(shapes), devices), 16) * 16


def reduce_kernel(shapes, slabs, chips, piece, factor, x_ref, *refs):
    outs = refs[: len(shapes)]
    from_pair, mine, landed, total, whole = refs[len(shapes) : len(shapes) + 5]
    pair_sems, send_sems, land_sems, back_send, back_land, fwd_send, fwd_land = refs[len(shapes) + 5 :]
    vol = lax.axis_index("vol")
    slab = lax.axis_index("slab")
    core = lax.rem(vol, 2)
    me = (vol // 2) * slabs + slab
    pair = (vol + 1 - 2 * core, slab)
    half = chips * piece

    def peer_of(step):
        other = lax.rem(me + step, chips)
        return ((other // slabs) * 2 + core, lax.rem(other, slabs))

    def rows_of(index):
        return pl.ds(pl.multiple_of(index * piece, 16), piece)

    barrier = pltpu.get_barrier_semaphore()
    pl.semaphore_signal(barrier, inc=1, device_id=pair, device_id_type=MESH)

    def greet(step, carry):
        pl.semaphore_signal(barrier, inc=1, device_id=peer_of(step), device_id_type=MESH)
        return carry

    lax.fori_loop(1, chips, greet, 0)
    pl.semaphore_wait(barrier, chips)

    swap = pltpu.make_async_remote_copy(
        src_ref=x_ref.at[pl.ds(pl.multiple_of((1 - core) * half, 16), half)],
        dst_ref=from_pair,
        send_sem=pair_sems.at[0],
        recv_sem=pair_sems.at[1],
        device_id=pair,
        device_id_type=MESH,
    )
    swap.start()
    swap.wait()
    own = x_ref[pl.ds(pl.multiple_of(core * half, 16), half), :].astype(jnp.float32)
    mine[...] = (own + from_pair[...].astype(jnp.float32)).astype(jnp.bfloat16)

    def scatter(step):
        other = lax.rem(me + step, chips)
        return pltpu.make_async_remote_copy(
            src_ref=mine.at[rows_of(other)],
            dst_ref=landed.at[rows_of(step)],
            send_sem=send_sems.at[step],
            recv_sem=land_sems.at[step],
            device_id=peer_of(step),
            device_id_type=MESH,
        )

    def start_scatter(step, carry):
        scatter(step).start()
        return carry

    lax.fori_loop(1, chips, start_scatter, 0)

    def add_landed(step, running):
        scatter(step).wait_recv()
        return running + landed[rows_of(step), :].astype(jnp.float32)

    summed = lax.fori_loop(1, chips, add_landed, mine[rows_of(me), :].astype(jnp.float32))
    total[...] = summed.astype(jnp.bfloat16)
    base = core * chips
    whole[rows_of(base + me), :] = total[...]

    def spread(step):
        return pltpu.make_async_remote_copy(
            src_ref=total,
            dst_ref=whole.at[rows_of(base + me)],
            send_sem=back_send.at[step],
            recv_sem=back_land.at[step],
            device_id=peer_of(step),
            device_id_type=MESH,
        )

    def start_spread(step, carry):
        spread(step).start()
        return carry

    lax.fori_loop(1, chips, start_spread, 0)

    def forward_on(step):
        index = base + lax.rem(me - step + chips, chips)
        return pltpu.make_async_remote_copy(
            src_ref=whole.at[rows_of(index)],
            dst_ref=whole.at[rows_of(index)],
            send_sem=fwd_send.at[step],
            recv_sem=fwd_land.at[step],
            device_id=pair,
            device_id_type=MESH,
        )

    forward_on(0).start()

    def hand_on(step, carry):
        spread(step).wait_recv()
        forward_on(step).start()
        return carry

    lax.fori_loop(1, chips, hand_on, 0)

    def settle(step, carry):
        forward_on(step).wait()
        return carry

    lax.fori_loop(0, chips, settle, 0)

    def drain(step, carry):
        scatter(step).wait_send()
        spread(step).wait_send()
        return carry

    lax.fori_loop(1, chips, drain, 0)
    for index, base_row, rows, start, width in tiles_of(shapes):
        tile = whole[base_row : base_row + rows, :].astype(jnp.float32) * factor
        outs[index][:, start : start + width] = tile[:, :width]


def reduce_all(packed, shapes, factor):
    slabs = lax.axis_size("slab")
    devices = lax.axis_size("vol") * slabs
    chips = devices // 2
    piece = piece_rows(shapes, devices)
    dma = pltpu.SemaphoreType.DMA
    return pl.pallas_call(
        functools.partial(reduce_kernel, shapes, slabs, chips, piece, factor),
        out_shape=[jax.ShapeDtypeStruct(shape, jnp.float32) for shape in shapes],
        in_specs=[pl.BlockSpec(memory_space=pltpu.VMEM)],
        out_specs=[pl.BlockSpec(memory_space=pltpu.VMEM)] * len(shapes),
        scratch_shapes=[
            pltpu.VMEM((chips * piece, 128), jnp.bfloat16),
            pltpu.VMEM((chips * piece, 128), jnp.bfloat16),
            pltpu.VMEM((chips * piece, 128), jnp.bfloat16),
            pltpu.VMEM((piece, 128), jnp.bfloat16),
            pltpu.VMEM((devices * piece, 128), jnp.bfloat16),
            dma((2,)),
            dma((chips,)),
            dma((chips,)),
            dma((chips,)),
            dma((chips,)),
            dma((chips,)),
            dma((chips,)),
        ],
        compiler_params=pltpu.CompilerParams(collective_id=0, has_side_effects=True),
        name="reduce_all",
    )(packed)


def pack(grads, rows):
    parts = []
    for grad in grads:
        wide = jnp.pad(grad, ((0, 0), (0, -grad.shape[1] % 128)))
        tiles = wide.reshape(grad.shape[0], -1, 128).transpose(1, 0, 2)
        parts.append(tiles.reshape(-1, 128))
    packed = jnp.concatenate(parts, axis=0)
    return jnp.pad(packed, ((0, rows - packed.shape[0]), (0, 0))).astype(jnp.bfloat16)


def per_device(volumes, w_first, w_second, w_third, map_grad):
    pads = ((1, 1), (1, 1), (1, 1))
    volume = lax.all_to_all(volumes, "slab", split_axis=0, concat_axis=2, tiled=True)
    pre_first = forward(volume, w_first, 2, pads)
    act_first = jax.nn.silu(pre_first).astype(jnp.bfloat16)
    pre_second = forward(act_first, w_second, 2, pads)
    act_second = jax.nn.silu(pre_second).astype(jnp.bfloat16)
    pre_third = forward(act_second, w_third, 1, pads)
    delta_third = (map_grad.astype(jnp.float32) * silu_slope(pre_third)).astype(jnp.bfloat16)
    grad_third = weight_grad(act_second, delta_third, 1, pads)
    back_second = interior(spread_back(delta_third, w_third, 1), act_second.shape)
    back_second = back_second.astype(jnp.bfloat16).astype(jnp.float32)
    delta_second = (back_second * silu_slope(pre_second)).astype(jnp.bfloat16)
    grad_second = weight_grad(act_first, delta_second, 2, pads)
    back_first = interior(spread_back(delta_second, w_second, 2), act_first.shape)
    delta_first = (back_first * silu_slope(pre_first)).astype(jnp.bfloat16)
    grad_first = weight_grad(volume, delta_first, 2, pads)
    grads = (grad_first, grad_second, grad_third)
    devices = lax.axis_size("vol") * lax.axis_size("slab")
    factor = 1.0 / (map_grad.shape[0] * devices)
    shapes = tuple(grad.shape for grad in grads)
    packed = pack(grads, devices * piece_rows(shapes, devices))
    return tuple(reduce_all(packed, shapes, factor))


def solution(mesh):
    return jax.shard_map(
        per_device,
        mesh=mesh,
        in_specs=(
            P("vol", None, "slab", None, None),
            P(),
            P(),
            P(),
            P(("vol", "slab"), None, None, None, None),
        ),
        out_specs=(P(), P(), P()),
        check_vma=False,
    )
```

```python
import functools

import jax
import jax.numpy as jnp
import numpy as np
from jax import lax
from jax.experimental import pallas as pl
from jax.experimental.pallas import tpu as pltpu
from jax.sharding import PartitionSpec as P

MESH = pl.DeviceIdType.MESH
BLOCK = 8


def one_hot(rows, cols, pairs):
    table = np.zeros((rows, cols), np.float32)
    for row, col in pairs:
        table[row, col] = 1.0
    return table


def cell_picks(depth, height, stride):
    out_depth, out_height = depth // stride, height // stride
    pairs = []
    for a in range(3):
        for b in range(3):
            for i in range(out_depth):
                for j in range(out_height):
                    z, y = stride * i + a - 1, stride * j + b - 1
                    if 0 <= z < depth and 0 <= y < height:
                        row = ((a * 3 + b) * out_depth + i) * out_height + j
                        pairs.append((row, z * height + y))
    return one_hot(9 * out_depth * out_height, depth * height, pairs)


def tables_of(channels, depth, height, width):
    blocks = width // (2 * BLOCK)
    spread = np.zeros((channels, width, blocks * 128), np.float32)
    for block in range(blocks):
        for at in range(2 * BLOCK + 1):
            x = 2 * BLOCK * block - 1 + at
            if x >= 0:
                for k in range(channels):
                    spread[k, x, block * 128 + at * channels + k] = 1.0
    taps = one_hot(
        27 * channels,
        9 * 128,
        [
            (pair * 3 * channels + lane, pair * 128 + lane)
            for pair in range(9)
            for lane in range(3 * channels)
        ],
    )
    plane, length = (depth // 4) * (height // 4), width // 4
    order = one_hot(
        plane * length,
        plane * length,
        [(l * plane + p, p * length + l) for l in range(length) for p in range(plane)],
    )
    second = cell_picks(depth // 2, height // 2, 2)
    third = cell_picks(depth // 4, height // 4, 1)
    tables = (spread, cell_picks(depth, height, 2), second, third, second.T, third.T, taps, order)
    return [jnp.asarray(table, jnp.bfloat16) for table in tables]


def contract(lhs, rhs, rhs_dim=0):
    return lax.dot_general(
        lhs, rhs, (((1,), (rhs_dim,)), ((), ())), preferred_element_type=jnp.float32
    )


def contract_fine(lhs, rhs):
    coarse = half(rhs)
    return contract(lhs, coarse) + contract(lhs, half(rhs - coarse.astype(jnp.float32)))


def sigmoid(pre):
    return 1.0 / (1.0 + jnp.exp(-pre))


def slope_of(pre):
    sigma = sigmoid(pre)
    return sigma * (1.0 + pre * (1.0 - sigma))


def half(value):
    return value.astype(jnp.bfloat16)


def sample_kernel(shapes, vol, w1, w2, w3, mg, spread, pick1, pick2, pick3, back2, back3, taps,
                  order, out, p1, p2, p3, w1b, w2p, w3p, a2, even3, odd3, even2, odd2, rows2, g2, g3):
    f32 = jnp.float32
    channels = vol.shape[0]
    c1, c2, c3 = w1.shape[0], w2.shape[0], w3.shape[0]
    blocks = spread.shape[2] // 128
    plane1, plane2 = pick1.shape[0] // 9, pick2.shape[0] // 9
    length2 = mg.shape[1] // plane2
    width1 = blocks * BLOCK * c1
    width2 = length2 * c2

    placed = contract(vol[0], spread[0])
    for k in range(1, channels):
        placed = placed + contract(vol[k], spread[k])
    r1 = half(contract(pick1[...], half(placed)))
    for pair in range(9):
        for block in range(blocks):
            p1[block * plane1 : (block + 1) * plane1, pair * 128 : (pair + 1) * 128] = r1[
                pair * plane1 : (pair + 1) * plane1, block * 128 : (block + 1) * 128
            ]
    wide = contract(w1[...], taps[...])
    for pair in range(9):
        tile = wide[:, pair * 128 : (pair + 1) * 128]
        for l in range(BLOCK):
            moved = pltpu.roll(tile, 2 * l * channels, 1) if l else tile
            w1b[l * c1 : (l + 1) * c1, pair * 128 : (pair + 1) * 128] = half(moved)
    w2p[...] = jnp.zeros_like(w2p)
    w3p[...] = jnp.zeros_like(w3p)
    for pair in range(9):
        w2p[:, pair * 128 : pair * 128 + 3 * c1] = w2[:, pair * 3 * c1 : (pair + 1) * 3 * c1]
        w3p[:, pair * 256 : pair * 256 + 3 * c2] = w3[:, pair * 3 * c2 : (pair + 1) * 3 * c2]

    pre1 = contract(p1[...], w1b[...], 1)
    act1 = half(pre1 * sigmoid(pre1))
    a1 = jnp.concatenate(
        [act1[block * plane1 : (block + 1) * plane1, :] for block in range(blocks)], axis=1
    )
    r2 = contract(pick2[...], a1)
    r2 = jnp.concatenate([r2, jnp.zeros((9 * plane2, 128), f32)], axis=1)
    sides = (half(pltpu.roll(r2, c1, 1)), half(pltpu.roll(r2, width1 + 128 - c1, 1)))
    for l in range(length2):
        chunk = sides[l % 2][:, (l // 2) * 128 : (l // 2 + 1) * 128]
        for pair in range(9):
            p2[l * plane2 : (l + 1) * plane2, pair * 128 : (pair + 1) * 128] = chunk[
                pair * plane2 : (pair + 1) * plane2, :
            ]
    pre2 = contract(p2[...], w2p[...], 1)
    act2 = pre2 * sigmoid(pre2)
    for l in range(length2):
        a2[:, l * c2 : (l + 1) * c2] = act2[l * plane2 : (l + 1) * plane2, :]
    r3 = contract(pick3[...], half(a2[...]))
    r3 = jnp.concatenate([r3, jnp.zeros((9 * plane2, 256), f32)], axis=1)
    sides = (half(pltpu.roll(r3, c2, 1)), half(r3))
    for l in range(length2):
        chunk = sides[l % 2][:, (l // 2) * 128 : (l // 2) * 128 + 256]
        for pair in range(9):
            p3[l * plane2 : (l + 1) * plane2, pair * 256 : (pair + 1) * 256] = chunk[
                pair * plane2 : (pair + 1) * plane2, :
            ]
    pre3 = contract(p3[...], w3p[...], 1)
    given = contract(order[...], mg[...], 1)
    slope3 = given * slope_of(pre3)
    delta3 = half(slope3)
    grad3 = contract(half(slope3.T), p3[...])
    g3[...] = jnp.zeros_like(g3)
    for pair in range(9):
        g3[:, pair * 3 * c2 : (pair + 1) * 3 * c2] = grad3[:, pair * 256 : pair * 256 + 3 * c2]

    spread3 = contract(delta3, w3p[...])
    for pair in range(9):
        for side, holder in ((0, even3), (1, odd3)):
            for tile in range(length2 // 2 + 1):
                total = None
                for part in range(2):
                    l = 2 * (tile - part) + side
                    if 0 <= l < length2:
                        piece = spread3[
                            l * plane2 : (l + 1) * plane2,
                            pair * 256 + part * 128 : pair * 256 + part * 128 + 128,
                        ]
                        total = piece if total is None else total + piece
                holder[pair * plane2 : (pair + 1) * plane2, tile * 128 : (tile + 1) * 128] = total
    down = contract_fine(back3[...], even3[...])
    down = pltpu.roll(down, down.shape[1] - c2, 1) + contract_fine(back3[...], odd3[...])
    for l in range(length2):
        rows2[l * plane2 : (l + 1) * plane2, :] = down[:, l * c2 : (l + 1) * c2]
    slope2 = half(rows2[...]).astype(f32) * slope_of(pre2)
    delta2 = half(slope2)
    grad2 = contract(half(slope2.T), p2[...])
    g2[...] = jnp.zeros_like(g2)
    for pair in range(9):
        g2[:, pair * 3 * c1 : (pair + 1) * 3 * c1] = grad2[:, pair * 128 : pair * 128 + 3 * c1]

    spread2 = contract(delta2, w2p[...])
    for pair in range(9):
        for l in range(length2):
            holder = odd2 if l % 2 else even2
            holder[pair * plane2 : (pair + 1) * plane2, (l // 2) * 128 : (l // 2 + 1) * 128] = spread2[
                l * plane2 : (l + 1) * plane2, pair * 128 : (pair + 1) * 128
            ]
    tail = jnp.zeros((plane1, 128), f32)
    left = jnp.concatenate([contract_fine(back2[...], even2[...]), tail], axis=1)
    right = jnp.concatenate([contract_fine(back2[...], odd2[...]), tail], axis=1)
    down = pltpu.roll(left, width1 + 128 - c1, 1) + pltpu.roll(right, c1, 1)
    step = BLOCK * c1
    down = jnp.concatenate([down[:, block * step : (block + 1) * step] for block in range(blocks)], axis=0)
    slope1 = down * slope_of(pre1)
    grad1 = contract(half(slope1.T), p1[...])
    tiles = []
    for pair in range(9):
        total = grad1[:c1, pair * 128 : (pair + 1) * 128]
        for l in range(1, BLOCK):
            tile = grad1[l * c1 : (l + 1) * c1, pair * 128 : (pair + 1) * 128]
            total = total + pltpu.roll(tile, 128 - 2 * l * channels, 1)
        tiles.append(half(total))
    first = contract(jnp.concatenate(tiles, axis=1), taps[...], 1)

    out[...] = jnp.zeros_like(out)
    grads = (first, g2, g3)
    for index, base, rows, start, width in tiles_of(shapes):
        if index == 0:
            out[base : base + rows, :width] = half(first)
        else:
            out[base : base + rows, :] = half(grads[index][:, start : start + 128])


def sample_grads(volume, w_first, w_second, w_third, map_grad, shapes, rows):
    channels, depth, height, width = volume.shape
    tables = tables_of(channels, depth, height, width)
    c1, c2, c3 = w_first.shape[0], w_second.shape[0], w_third.shape[0]
    plane1 = depth * height // 4
    plane2 = depth * height // 16
    length2 = width // 4
    cells = plane2 * length2
    bf16, f32 = jnp.bfloat16, jnp.float32
    scratch = [
        ((width // (2 * BLOCK) * plane1, 9 * 128), bf16),
        ((cells, 9 * 128), bf16),
        ((cells, 9 * 256), bf16),
        ((BLOCK * c1, 9 * 128), bf16),
        ((c2, 9 * 128), bf16),
        ((c3, 9 * 256), bf16),
        ((plane2, length2 * c2), f32),
        ((9 * plane2, length2 * c2 + 128), f32),
        ((9 * plane2, length2 * c2 + 128), f32),
        ((9 * plane2, width // 2 * c1), f32),
        ((9 * plane2, width // 2 * c1), f32),
        ((cells, c2), f32),
        ((c2, pl.cdiv(27 * c1, 128) * 128), f32),
        ((c3, pl.cdiv(27 * c2, 128) * 128), f32),
    ]
    operands = (
        volume.reshape(channels, depth * height, width),
        w_first,
        w_second,
        w_third,
        map_grad.reshape(c3, cells),
        *tables,
    )
    return pl.pallas_call(
        functools.partial(sample_kernel, shapes),
        out_shape=jax.ShapeDtypeStruct((rows, 128), bf16),
        in_specs=[pl.BlockSpec(memory_space=pltpu.VMEM)] * len(operands),
        out_specs=pl.BlockSpec(memory_space=pltpu.VMEM),
        scratch_shapes=[pltpu.VMEM(shape, kind) for shape, kind in scratch],
        compiler_params=pltpu.CompilerParams(vmem_limit_bytes=56 << 20),
        name="sample_grads",
    )(*operands)


def packed_rows(shapes):
    return sum(pl.cdiv(cols, 128) * rows for rows, cols in shapes)


def tiles_of(shapes):
    base = 0
    for index, (rows, cols) in enumerate(shapes):
        for start in range(0, cols, 128):
            yield index, base, rows, start, min(128, cols - start)
            base += rows


def piece_rows(shapes, devices):
    return pl.cdiv(pl.cdiv(packed_rows(shapes), devices), 16) * 16


def reduce_kernel(shapes, slabs, chips, piece, factor, x_ref, *refs):
    outs = refs[: len(shapes)]
    from_pair, mine, landed, total, whole = refs[len(shapes) : len(shapes) + 5]
    pair_sems, send_sems, land_sems, back_send, back_land, fwd_send, fwd_land = refs[len(shapes) + 5 :]
    vol = lax.axis_index("vol")
    slab = lax.axis_index("slab")
    core = lax.rem(vol, 2)
    me = (vol // 2) * slabs + slab
    pair = (vol + 1 - 2 * core, slab)
    half = chips * piece

    def peer_of(step):
        other = lax.rem(me + step, chips)
        return ((other // slabs) * 2 + core, lax.rem(other, slabs))

    def rows_of(index):
        return pl.ds(pl.multiple_of(index * piece, 16), piece)

    barrier = pltpu.get_barrier_semaphore()
    pl.semaphore_signal(barrier, inc=1, device_id=pair, device_id_type=MESH)

    def greet(step, carry):
        pl.semaphore_signal(barrier, inc=1, device_id=peer_of(step), device_id_type=MESH)
        return carry

    lax.fori_loop(1, chips, greet, 0)
    pl.semaphore_wait(barrier, chips)

    swap = pltpu.make_async_remote_copy(
        src_ref=x_ref.at[pl.ds(pl.multiple_of((1 - core) * half, 16), half)],
        dst_ref=from_pair,
        send_sem=pair_sems.at[0],
        recv_sem=pair_sems.at[1],
        device_id=pair,
        device_id_type=MESH,
    )
    swap.start()
    swap.wait()
    own = x_ref[pl.ds(pl.multiple_of(core * half, 16), half), :].astype(jnp.float32)
    mine[...] = (own + from_pair[...].astype(jnp.float32)).astype(jnp.bfloat16)

    def scatter(step):
        other = lax.rem(me + step, chips)
        return pltpu.make_async_remote_copy(
            src_ref=mine.at[rows_of(other)],
            dst_ref=landed.at[rows_of(step)],
            send_sem=send_sems.at[step],
            recv_sem=land_sems.at[step],
            device_id=peer_of(step),
            device_id_type=MESH,
        )

    def start_scatter(step, carry):
        scatter(step).start()
        return carry

    lax.fori_loop(1, chips, start_scatter, 0)

    def add_landed(step, running):
        scatter(step).wait_recv()
        return running + landed[rows_of(step), :].astype(jnp.float32)

    summed = lax.fori_loop(1, chips, add_landed, mine[rows_of(me), :].astype(jnp.float32))
    total[...] = summed.astype(jnp.bfloat16)
    base = core * chips
    whole[rows_of(base + me), :] = total[...]

    def spread(step):
        return pltpu.make_async_remote_copy(
            src_ref=total,
            dst_ref=whole.at[rows_of(base + me)],
            send_sem=back_send.at[step],
            recv_sem=back_land.at[step],
            device_id=peer_of(step),
            device_id_type=MESH,
        )

    def start_spread(step, carry):
        spread(step).start()
        return carry

    lax.fori_loop(1, chips, start_spread, 0)

    def forward_on(step):
        index = base + lax.rem(me - step + chips, chips)
        return pltpu.make_async_remote_copy(
            src_ref=whole.at[rows_of(index)],
            dst_ref=whole.at[rows_of(index)],
            send_sem=fwd_send.at[step],
            recv_sem=fwd_land.at[step],
            device_id=pair,
            device_id_type=MESH,
        )

    forward_on(0).start()

    def hand_on(step, carry):
        spread(step).wait_recv()
        forward_on(step).start()
        return carry

    lax.fori_loop(1, chips, hand_on, 0)

    def settle(step, carry):
        forward_on(step).wait()
        return carry

    lax.fori_loop(0, chips, settle, 0)

    def drain(step, carry):
        scatter(step).wait_send()
        spread(step).wait_send()
        return carry

    lax.fori_loop(1, chips, drain, 0)
    for index, base_row, rows, start, width in tiles_of(shapes):
        tile = whole[base_row : base_row + rows, :].astype(jnp.float32) * factor
        outs[index][:, start : start + width] = tile[:, :width]


def reduce_all(packed, shapes, factor):
    slabs = lax.axis_size("slab")
    devices = lax.axis_size("vol") * slabs
    chips = devices // 2
    piece = piece_rows(shapes, devices)
    dma = pltpu.SemaphoreType.DMA
    return pl.pallas_call(
        functools.partial(reduce_kernel, shapes, slabs, chips, piece, factor),
        out_shape=[jax.ShapeDtypeStruct(shape, jnp.float32) for shape in shapes],
        in_specs=[pl.BlockSpec(memory_space=pltpu.VMEM)],
        out_specs=[pl.BlockSpec(memory_space=pltpu.VMEM)] * len(shapes),
        scratch_shapes=[
            pltpu.VMEM((chips * piece, 128), jnp.bfloat16),
            pltpu.VMEM((chips * piece, 128), jnp.bfloat16),
            pltpu.VMEM((chips * piece, 128), jnp.bfloat16),
            pltpu.VMEM((piece, 128), jnp.bfloat16),
            pltpu.VMEM((devices * piece, 128), jnp.bfloat16),
            dma((2,)),
            dma((chips,)),
            dma((chips,)),
            dma((chips,)),
            dma((chips,)),
            dma((chips,)),
            dma((chips,)),
        ],
        compiler_params=pltpu.CompilerParams(collective_id=0, has_side_effects=True),
        name="reduce_all",
    )(packed)


def per_device(volumes, w_first, w_second, w_third, map_grad):
    volume = lax.all_to_all(volumes, "slab", split_axis=0, concat_axis=2, tiled=True)
    devices = lax.axis_size("vol") * lax.axis_size("slab")
    factor = 1.0 / (map_grad.shape[0] * devices)
    shapes = (w_first.shape, w_second.shape, w_third.shape)
    rows = devices * piece_rows(shapes, devices)
    packed = sample_grads(volume[0], w_first, w_second, w_third, map_grad[0], shapes, rows)
    return tuple(reduce_all(packed, shapes, factor))


def solution(mesh):
    return jax.shard_map(
        per_device,
        mesh=mesh,
        in_specs=(
            P("vol", None, "slab", None, None),
            P(),
            P(),
            P(),
            P(("vol", "slab"), None, None, None, None),
        ),
        out_specs=(P(), P(), P()),
        check_vma=False,
    )
```

```python
import functools

import jax
import jax.numpy as jnp
import numpy as np
from jax import lax
from jax.experimental import pallas as pl
from jax.experimental.pallas import tpu as pltpu
from jax.sharding import PartitionSpec as P

MESH = pl.DeviceIdType.MESH
BLOCK = 8


def one_hot(rows, cols, pairs):
    table = np.zeros((rows, cols), np.float32)
    for row, col in pairs:
        table[row, col] = 1.0
    return table


def cell_picks(depth, height, stride):
    out_depth, out_height = depth // stride, height // stride
    pairs = []
    for a in range(3):
        for b in range(3):
            for i in range(out_depth):
                for j in range(out_height):
                    z, y = stride * i + a - 1, stride * j + b - 1
                    if 0 <= z < depth and 0 <= y < height:
                        row = ((a * 3 + b) * out_depth + i) * out_height + j
                        pairs.append((row, z * height + y))
    return one_hot(9 * out_depth * out_height, depth * height, pairs)


def tables_of(channels, depth, height, width):
    blocks = width // (2 * BLOCK)
    spread = np.zeros((channels, width, blocks * 128), np.float32)
    for block in range(blocks):
        for at in range(2 * BLOCK + 1):
            x = 2 * BLOCK * block - 1 + at
            if x >= 0:
                for k in range(channels):
                    spread[k, x, block * 128 + at * channels + k] = 1.0
    taps = one_hot(
        27 * channels,
        9 * 128,
        [
            (pair * 3 * channels + lane, pair * 128 + lane)
            for pair in range(9)
            for lane in range(3 * channels)
        ],
    )
    plane, length = (depth // 4) * (height // 4), width // 4
    order = one_hot(
        plane * length,
        plane * length,
        [(l * plane + p, p * length + l) for l in range(length) for p in range(plane)],
    )
    second = cell_picks(depth // 2, height // 2, 2)
    third = cell_picks(depth // 4, height // 4, 1)
    tables = (spread, cell_picks(depth, height, 2), second, third, second.T, third.T, taps, order)
    return [jnp.asarray(table, jnp.bfloat16) for table in tables]


def contract(lhs, rhs, rhs_dim=0):
    return lax.dot_general(
        lhs, rhs, (((1,), (rhs_dim,)), ((), ())), preferred_element_type=jnp.float32
    )


def contract_fine(lhs, rhs):
    coarse = half(rhs)
    return contract(lhs, coarse) + contract(lhs, half(rhs - coarse.astype(jnp.float32)))


def sigmoid(pre):
    return 1.0 / (1.0 + jnp.exp(-pre))


def slope_of(pre):
    sigma = sigmoid(pre)
    return sigma * (1.0 + pre * (1.0 - sigma))


def half(value):
    return value.astype(jnp.bfloat16)


def packed_rows(shapes):
    return sum(pl.cdiv(cols, 128) * rows for rows, cols in shapes)


def tiles_of(shapes):
    base = 0
    for index, (rows, cols) in enumerate(shapes):
        for start in range(0, cols, 128):
            yield index, base, rows, start, min(128, cols - start)
            base += rows


def piece_rows(shapes, devices):
    return pl.cdiv(pl.cdiv(packed_rows(shapes), devices), 16) * 16


class Exchange:
    def __init__(self, source, held, sems, slabs, ring):
        self.slabs = slabs
        self.source, self.held, self.sems = source, held, sems
        self.vol, self.slab = ring.vol, ring.slab

    def copy(self, step):
        other = lax.rem(self.slab + step, self.slabs)
        return pltpu.make_async_remote_copy(
            src_ref=self.source.at[other],
            dst_ref=self.held.at[self.slab],
            send_sem=self.sems.at[0, step],
            recv_sem=self.sems.at[1, step],
            device_id=(self.vol, other),
            device_id_type=MESH,
        )

    def start(self):
        for step in range(1, self.slabs):
            self.copy(step).start()
        self.held[self.slab] = self.source[self.slab]

    def wait_all(self):
        for step in range(1, self.slabs):
            self.copy(step).wait_recv()

    def drain(self):
        for step in range(1, self.slabs):
            self.copy(step).wait_send()


class Ring:
    def __init__(self, slabs, chips):
        self.slabs, self.chips = slabs, chips
        self.vol = lax.axis_index("vol")
        self.slab = lax.axis_index("slab")
        self.core = lax.rem(self.vol, 2)
        self.me = (self.vol // 2) * slabs + self.slab
        self.pair = (self.vol + 1 - 2 * self.core, self.slab)

    def peer(self, step):
        other = lax.rem(self.me + step, self.chips)
        return ((other // self.slabs) * 2 + self.core, lax.rem(other, self.slabs))

    def steps(self, action, first=1):
        def body(step, carry):
            action(step)
            return carry

        lax.fori_loop(first, self.chips, body, 0)

    def greet(self):
        barrier = pltpu.get_barrier_semaphore()
        pl.semaphore_signal(barrier, inc=1, device_id=self.pair, device_id_type=MESH)
        self.steps(
            lambda step: pl.semaphore_signal(
                barrier, inc=1, device_id=self.peer(step), device_id_type=MESH
            )
        )
        pl.semaphore_wait(barrier, self.chips)


class Summed:
    def __init__(self, ring, own, from_pair, mine, landed, total, whole, pair_sems, sems):
        self.ring = ring
        self.own, self.from_pair, self.mine = own, from_pair, mine
        self.landed, self.total, self.whole = landed, total, whole
        self.pair_sems, self.sems = pair_sems, sems
        self.piece = total.shape[0]
        self.half = ring.chips * self.piece
        self.base = ring.core * ring.chips

    def rows(self, index):
        return pl.ds(pl.multiple_of(index * self.piece, 16), self.piece)

    def halves(self, index):
        return pl.ds(pl.multiple_of(index * self.half, 16), self.half)

    def remote(self, source, target, kind, step, device):
        return pltpu.make_async_remote_copy(
            src_ref=source,
            dst_ref=target,
            send_sem=self.sems.at[kind, 0, step],
            recv_sem=self.sems.at[kind, 1, step],
            device_id=device,
            device_id_type=MESH,
        )

    def swap(self):
        return pltpu.make_async_remote_copy(
            src_ref=self.own.at[self.halves(1 - self.ring.core)],
            dst_ref=self.from_pair,
            send_sem=self.pair_sems.at[0],
            recv_sem=self.pair_sems.at[1],
            device_id=self.ring.pair,
            device_id_type=MESH,
        )

    def outward(self, step):
        other = lax.rem(self.ring.me + step, self.ring.chips)
        source, target = self.mine.at[self.rows(other)], self.landed.at[self.rows(step)]
        return self.remote(source, target, 0, step, self.ring.peer(step))

    def back(self, step):
        target = self.whole.at[self.rows(self.base + self.ring.me)]
        return self.remote(self.total, target, 1, step, self.ring.peer(step))

    def across(self, step):
        chips = self.ring.chips
        block = self.whole.at[self.rows(self.base + lax.rem(self.ring.me - step + chips, chips))]
        return self.remote(block, block, 2, step, self.ring.pair)

    def scatter(self):
        self.swap().wait()
        own = self.own[self.halves(self.ring.core), :].astype(jnp.float32)
        self.mine[...] = half(own + self.from_pair[...].astype(jnp.float32))
        self.ring.steps(lambda step: self.outward(step).start())

    def gather(self):
        def add(step, running):
            self.outward(step).wait_recv()
            return running + self.landed[self.rows(step), :].astype(jnp.float32)

        start = self.mine[self.rows(self.ring.me), :].astype(jnp.float32)
        self.total[...] = half(lax.fori_loop(1, self.ring.chips, add, start))
        self.whole[self.rows(self.base + self.ring.me), :] = self.total[...]
        self.ring.steps(lambda step: self.back(step).start())

    def hand_on(self):
        self.across(0).start()

        def pass_on(step):
            self.back(step).wait_recv()
            self.across(step).start()

        self.ring.steps(pass_on)

    def settle(self):
        self.ring.steps(lambda step: self.across(step).wait(), 0)

        def drain(step):
            self.outward(step).wait_send()
            self.back(step).wait_send()

        self.ring.steps(drain)


def step_kernel(shapes, slabs, chips, volumes, w1, w2, w3, mg, spread, pick1, pick2, pick3, back2,
                back3, taps, order, out, p1, p2, p3, w1b, w2p, w3p, a2, even3, odd3, even2, odd2,
                rows2, g2, vol, vol_sems, *parts):
    ring = Ring(slabs, chips)
    ring.greet()
    incoming = Exchange(volumes, vol, vol_sems, slabs, ring)
    incoming.start()
    late, early = Summed(ring, *parts[:8]), Summed(ring, *parts[8:])
    late.own[...] = jnp.zeros_like(late.own)
    early.own[...] = jnp.zeros_like(early.own)

    f32 = jnp.float32
    channels = vol.shape[1]
    c1, c2 = w1.shape[0], w2.shape[0]
    blocks = spread.shape[2] // 128
    plane1, plane2 = pick1.shape[0] // 9, pick2.shape[0] // 9
    length2 = mg.shape[0] // plane2
    width1 = blocks * BLOCK * c1
    width2 = length2 * c2

    wide = contract(w1[...], taps[...])
    for pair in range(9):
        tile = wide[:, pair * 128 : (pair + 1) * 128]
        for l in range(BLOCK):
            moved = pltpu.roll(tile, 2 * l * channels, 1) if l else tile
            w1b[l * c1 : (l + 1) * c1, pair * 128 : (pair + 1) * 128] = half(moved)
    w2p[...] = jnp.zeros_like(w2p)
    w3p[...] = jnp.zeros_like(w3p)
    for pair in range(9):
        w2p[:, pair * 128 : pair * 128 + 3 * c1] = w2[:, pair * 3 * c1 : (pair + 1) * 3 * c1]
        w3p[pair * 256 : pair * 256 + 3 * c2, :] = w3[pair * 3 * c2 : (pair + 1) * 3 * c2, :]

    incoming.wait_all()
    levels = []
    for part in range(vol.shape[0]):
        placed = contract(vol[part, 0], spread[0])
        for k in range(1, channels):
            placed = placed + contract(vol[part, k], spread[k])
        levels.append(half(placed))
    r1 = half(contract(pick1[...], jnp.concatenate(levels, axis=0)))
    for pair in range(9):
        for block in range(blocks):
            p1[block * plane1 : (block + 1) * plane1, pair * 128 : (pair + 1) * 128] = r1[
                pair * plane1 : (pair + 1) * plane1, block * 128 : (block + 1) * 128
            ]
    pre1 = contract(p1[...], w1b[...], 1)
    act1 = half(pre1 * sigmoid(pre1))
    a1 = jnp.concatenate(
        [act1[block * plane1 : (block + 1) * plane1, :] for block in range(blocks)], axis=1
    )
    r2 = contract(pick2[...], a1)
    r2 = jnp.concatenate([r2, jnp.zeros((9 * plane2, 128), f32)], axis=1)
    sides = (half(pltpu.roll(r2, c1, 1)), half(pltpu.roll(r2, width1 + 128 - c1, 1)))
    for l in range(length2):
        chunk = sides[l % 2][:, (l // 2) * 128 : (l // 2 + 1) * 128]
        for pair in range(9):
            p2[l * plane2 : (l + 1) * plane2, pair * 128 : (pair + 1) * 128] = chunk[
                pair * plane2 : (pair + 1) * plane2, :
            ]
    pre2 = contract(p2[...], w2p[...], 1)
    act2 = pre2 * sigmoid(pre2)
    for l in range(length2):
        a2[:, l * c2 : (l + 1) * c2] = act2[l * plane2 : (l + 1) * plane2, :]
    r3 = contract(pick3[...], half(a2[...]))
    r3 = jnp.concatenate([r3, jnp.zeros((9 * plane2, 256), f32)], axis=1)
    sides = (half(pltpu.roll(r3, c2, 1)), half(r3))
    for l in range(length2):
        chunk = sides[l % 2][:, (l // 2) * 128 : (l // 2) * 128 + 256]
        for pair in range(9):
            p3[l * plane2 : (l + 1) * plane2, pair * 256 : (pair + 1) * 256] = chunk[
                pair * plane2 : (pair + 1) * plane2, :
            ]
    pre3 = contract(p3[...], w3p[...])
    given = contract(order[...], mg[...])
    slope3 = given * slope_of(pre3)
    delta3 = half(slope3)
    grad3 = contract(half(slope3.T), p3[...])
    for pair in range(9):
        for lane in range(0, 3 * c2, 128):
            wide = min(128, 3 * c2 - lane)
            turned = grad3[:, pair * 256 + lane : pair * 256 + lane + 128].T
            at = pair * 3 * c2 + lane
            late.own[at : at + wide, :] = half(turned[:wide, :])
    late.swap().start()

    spread3 = contract(delta3, w3p[...], 1)
    for pair in range(9):
        for side, holder in ((0, even3), (1, odd3)):
            for tile in range(length2 // 2 + 1):
                total = None
                for part in range(2):
                    l = 2 * (tile - part) + side
                    if 0 <= l < length2:
                        piece = spread3[
                            l * plane2 : (l + 1) * plane2,
                            pair * 256 + part * 128 : pair * 256 + part * 128 + 128,
                        ]
                        total = piece if total is None else total + piece
                holder[pair * plane2 : (pair + 1) * plane2, tile * 128 : (tile + 1) * 128] = total
    down = contract_fine(back3[...], even3[...])
    down = pltpu.roll(down, down.shape[1] - c2, 1) + contract_fine(back3[...], odd3[...])
    for l in range(length2):
        rows2[l * plane2 : (l + 1) * plane2, :] = down[:, l * c2 : (l + 1) * c2]
    slope2 = half(rows2[...]).astype(f32) * slope_of(pre2)
    delta2 = half(slope2)
    late.scatter()
    grad2 = contract(half(slope2.T), p2[...])
    g2[...] = jnp.zeros_like(g2)
    for pair in range(9):
        g2[:, pair * 3 * c1 : (pair + 1) * 3 * c1] = grad2[:, pair * 128 : pair * 128 + 3 * c1]

    spread2 = contract(delta2, w2p[...])
    for pair in range(9):
        for l in range(length2):
            holder = odd2 if l % 2 else even2
            holder[pair * plane2 : (pair + 1) * plane2, (l // 2) * 128 : (l // 2 + 1) * 128] = spread2[
                l * plane2 : (l + 1) * plane2, pair * 128 : (pair + 1) * 128
            ]
    tail = jnp.zeros((plane1, 128), f32)
    left = jnp.concatenate([contract_fine(back2[...], even2[...]), tail], axis=1)
    right = jnp.concatenate([contract_fine(back2[...], odd2[...]), tail], axis=1)
    down = pltpu.roll(left, width1 + 128 - c1, 1) + pltpu.roll(right, c1, 1)
    step = BLOCK * c1
    down = jnp.concatenate([down[:, block * step : (block + 1) * step] for block in range(blocks)], axis=0)
    slope1 = down * slope_of(pre1)
    grad1 = contract(half(slope1.T), p1[...])
    tiles = []
    for pair in range(9):
        total = grad1[:c1, pair * 128 : (pair + 1) * 128]
        for l in range(1, BLOCK):
            tile = grad1[l * c1 : (l + 1) * c1, pair * 128 : (pair + 1) * 128]
            total = total + pltpu.roll(tile, 128 - 2 * l * channels, 1)
        tiles.append(half(total))
    first = contract(jnp.concatenate(tiles, axis=1), taps[...], 1)

    for index, base, rows, start, width in tiles_of(shapes[:2]):
        if index == 0:
            early.own[base : base + rows, :width] = half(first)
        else:
            early.own[base : base + rows, :] = half(g2[:, start : start + 128])
    early.swap().start()
    late.gather()
    early.scatter()
    late.hand_on()
    early.gather()
    early.hand_on()
    late.settle()
    early.settle()
    incoming.drain()
    out[: late.whole.shape[0], :] = late.whole[...]
    out[late.whole.shape[0] :, :] = early.whole[...]


def unpack_kernel(shapes, bases, factor, packed, first, second, third):
    for out, shape, base in ((first, shapes[:1], bases[0]), (second, shapes[1:2], bases[1])):
        for index, at, rows, start, width in tiles_of(shape):
            tile = packed[base + at : base + at + rows, :].astype(jnp.float32) * factor
            out[:, start : start + width] = tile[:, :width]
    third[...] = packed[: third.shape[0], :].astype(jnp.float32) * factor


def per_device(volumes, w_first, w_second, w_third, map_grad):
    slabs = lax.axis_size("slab")
    devices = lax.axis_size("vol") * slabs
    chips = devices // 2
    factor = 1.0 / (map_grad.shape[0] * devices)
    shapes = (w_first.shape, w_second.shape, w_third.shape)
    parts, channels, level, height, width = volumes.shape
    depth = level * slabs
    tables = tables_of(channels, depth, height, width)
    c1, c2, c3 = w_first.shape[0], w_second.shape[0], w_third.shape[0]
    plane1 = depth * height // 4
    plane2 = depth * height // 16
    length2 = width // 4
    cells = plane2 * length2
    bf16, f32 = jnp.bfloat16, jnp.float32
    late_piece = piece_rows(((27 * c2, c3),), devices)
    early_piece = piece_rows(shapes[:2], devices)
    scratch = [
        ((width // (2 * BLOCK) * plane1, 9 * 128), bf16),
        ((cells, 9 * 128), bf16),
        ((cells, 9 * 256), bf16),
        ((BLOCK * c1, 9 * 128), bf16),
        ((c2, 9 * 128), bf16),
        ((9 * 256, c3), bf16),
        ((plane2, length2 * c2), f32),
        ((9 * plane2, length2 * c2 + 128), f32),
        ((9 * plane2, length2 * c2 + 128), f32),
        ((9 * plane2, width // 2 * c1), f32),
        ((9 * plane2, width // 2 * c1), f32),
        ((cells, c2), f32),
        ((c2, pl.cdiv(27 * c1, 128) * 128), f32),
        ((slabs, channels, level * height, width), bf16),
    ]
    scratch = [pltpu.VMEM(shape, kind) for shape, kind in scratch]
    dma = pltpu.SemaphoreType.DMA
    scratch.append(dma((2, slabs)))
    for piece in (late_piece, early_piece):
        for count in (devices, chips, chips, chips, 1, devices):
            scratch.append(pltpu.VMEM((count * piece, 128), bf16))
        scratch += [dma((2,)), dma((3, 2, chips))]
    operands = (
        volumes.reshape(parts, channels, level * height, width),
        w_first,
        w_second,
        w_third.T,
        map_grad[0].transpose(1, 2, 3, 0).reshape(cells, c3),
        *tables,
    )
    in_vmem = pl.BlockSpec(memory_space=pltpu.VMEM)
    packed = pl.pallas_call(
        functools.partial(step_kernel, shapes, slabs, chips),
        out_shape=jax.ShapeDtypeStruct((devices * (late_piece + early_piece), 128), bf16),
        in_specs=[in_vmem] * len(operands),
        out_specs=in_vmem,
        scratch_shapes=scratch,
        compiler_params=pltpu.CompilerParams(
            collective_id=0, has_side_effects=True, vmem_limit_bytes=56 << 20
        ),
        name="step",
    )(*operands)
    early_base = devices * late_piece
    bases = (early_base, early_base + packed_rows(shapes[:1]))
    outs = (shapes[0], shapes[1], (27 * c2, c3))
    first, second, third = pl.pallas_call(
        functools.partial(unpack_kernel, shapes, bases, factor),
        out_shape=[jax.ShapeDtypeStruct(shape, f32) for shape in outs],
        in_specs=[in_vmem],
        out_specs=[in_vmem] * 3,
        name="unpack",
    )(packed)
    return first, second, third.T


def solution(mesh):
    return jax.shard_map(
        per_device,
        mesh=mesh,
        in_specs=(
            P("vol", None, "slab", None, None),
            P(),
            P(),
            P(),
            P(("vol", "slab"), None, None, None, None),
        ),
        out_specs=(P(), P(), P()),
        check_vma=False,
    )
```

```python
import functools

import jax
import jax.numpy as jnp
import numpy as np
from jax import lax
from jax.experimental import pallas as pl
from jax.experimental.pallas import tpu as pltpu
from jax.sharding import PartitionSpec as P

MESH = pl.DeviceIdType.MESH
BLOCK = 8


def one_hot(rows, cols, pairs):
    table = np.zeros((rows, cols), np.float32)
    for row, col in pairs:
        table[row, col] = 1.0
    return table


def cell_picks(depth, height, stride):
    out_depth, out_height = depth // stride, height // stride
    pairs = []
    for a in range(3):
        for b in range(3):
            for i in range(out_depth):
                for j in range(out_height):
                    z, y = stride * i + a - 1, stride * j + b - 1
                    if 0 <= z < depth and 0 <= y < height:
                        row = ((a * 3 + b) * out_depth + i) * out_height + j
                        pairs.append((row, z * height + y))
    return one_hot(9 * out_depth * out_height, depth * height, pairs)


def tables_of(channels, depth, height, width):
    blocks = width // (2 * BLOCK)
    spread = np.zeros((channels, width, blocks * 128), np.float32)
    for block in range(blocks):
        for at in range(2 * BLOCK + 1):
            x = 2 * BLOCK * block - 1 + at
            if x >= 0:
                for k in range(channels):
                    spread[k, x, block * 128 + at * channels + k] = 1.0
    taps = one_hot(
        27 * channels,
        9 * 128,
        [
            (pair * 3 * channels + lane, pair * 128 + lane)
            for pair in range(9)
            for lane in range(3 * channels)
        ],
    )
    plane, length = (depth // 4) * (height // 4), width // 4
    order = one_hot(
        plane * length,
        plane * length,
        [(l * plane + p, p * length + l) for l in range(length) for p in range(plane)],
    )
    second = cell_picks(depth // 2, height // 2, 2)
    third = cell_picks(depth // 4, height // 4, 1)
    tables = (spread, cell_picks(depth, height, 2), second, third, second.T, third.T, taps, order)
    return [jnp.asarray(table, jnp.bfloat16) for table in tables]


def contract(lhs, rhs, rhs_dim=0):
    return lax.dot_general(
        lhs, rhs, (((1,), (rhs_dim,)), ((), ())), preferred_element_type=jnp.float32
    )


def contract_fine(lhs, rhs):
    coarse = half(rhs)
    return contract(lhs, coarse) + contract(lhs, half(rhs - coarse.astype(jnp.float32)))


def sigmoid(pre):
    return 1.0 / (1.0 + jnp.exp(-pre))


def slope_of(pre):
    sigma = sigmoid(pre)
    return sigma * (1.0 + pre * (1.0 - sigma))


def half(value):
    return value.astype(jnp.bfloat16)


def packed_rows(shapes):
    return sum(pl.cdiv(cols, 128) * rows for rows, cols in shapes)


def tiles_of(shapes):
    base = 0
    for index, (rows, cols) in enumerate(shapes):
        for start in range(0, cols, 128):
            yield index, base, rows, start, min(128, cols - start)
            base += rows


def piece_rows(shapes, devices):
    return pl.cdiv(pl.cdiv(packed_rows(shapes), devices), 16) * 16


class Exchange:
    def __init__(self, source, held, sems, slabs, ring):
        self.slabs = slabs
        self.source, self.held, self.sems = source, held, sems
        self.vol, self.slab = ring.vol, ring.slab

    def copy(self, step):
        other = lax.rem(self.slab + step, self.slabs)
        return pltpu.make_async_remote_copy(
            src_ref=self.source.at[other],
            dst_ref=self.held.at[self.slab],
            send_sem=self.sems.at[0, step],
            recv_sem=self.sems.at[1, step],
            device_id=(self.vol, other),
            device_id_type=MESH,
        )

    def start(self):
        for step in range(1, self.slabs):
            self.copy(step).start()
        self.held[self.slab] = self.source[self.slab]

    def wait_all(self):
        for step in range(1, self.slabs):
            self.copy(step).wait_recv()

    def drain(self):
        for step in range(1, self.slabs):
            self.copy(step).wait_send()


class Ring:
    def __init__(self, slabs, lines):
        self.slabs, self.lines, self.planes = slabs, lines, 2 * slabs
        self.vol = lax.axis_index("vol")
        self.slab = lax.axis_index("slab")
        self.core = lax.rem(self.vol, 2)
        self.side = lax.rem(self.vol // 2, 2)
        self.at_line = self.vol // 4
        self.at_plane = self.side * slabs + self.slab
        self.pair = (self.vol + 1 - 2 * self.core, self.slab)

    def in_plane(self, step):
        other = lax.rem(self.at_plane + step, self.planes)
        vol = (self.at_line * 2 + other // self.slabs) * 2 + self.core
        return other, (vol, lax.rem(other, self.slabs))

    def in_line(self, step):
        other = lax.rem(self.at_line + step, self.lines)
        return other, ((other * 2 + self.side) * 2 + self.core, self.slab)

    def greet(self):
        barrier = pltpu.get_barrier_semaphore()
        partners = [self.pair]
        partners += [self.in_plane(step)[1] for step in range(1, self.planes)]
        partners += [self.in_line(step)[1] for step in range(1, self.lines)]
        for partner in partners:
            pl.semaphore_signal(barrier, inc=1, device_id=partner, device_id_type=MESH)
        pl.semaphore_wait(barrier, len(partners))


class Summed:
    def __init__(self, ring, own, from_pair, mine, landed, middle, lined, total, whole, *sems):
        self.ring = ring
        self.own, self.from_pair, self.mine = own, from_pair, mine
        self.landed, self.middle, self.lined = landed, middle, lined
        self.total, self.whole = total, whole
        self.pair_sems, self.plane_sems, self.line_sems = sems
        self.piece = total.shape[0]
        self.block = ring.lines * self.piece
        self.half = ring.planes * self.block
        self.spot = ring.core * ring.planes + ring.at_plane

    def pieces(self, index):
        return pl.ds(pl.multiple_of(index * self.piece, 16), self.piece)

    def blocks(self, index):
        return pl.ds(pl.multiple_of(index * self.block, 16), self.block)

    def halves(self, index):
        return pl.ds(pl.multiple_of(index * self.half, 16), self.half)

    def remote(self, source, target, sems, kind, step, device):
        return pltpu.make_async_remote_copy(
            src_ref=source,
            dst_ref=target,
            send_sem=sems.at[kind, 0, step],
            recv_sem=sems.at[kind, 1, step],
            device_id=device,
            device_id_type=MESH,
        )

    def swap(self):
        return pltpu.make_async_remote_copy(
            src_ref=self.own.at[self.halves(1 - self.ring.core)],
            dst_ref=self.from_pair,
            send_sem=self.pair_sems.at[0],
            recv_sem=self.pair_sems.at[1],
            device_id=self.ring.pair,
            device_id_type=MESH,
        )

    def plane_out(self, step):
        other, device = self.ring.in_plane(step)
        source, target = self.mine.at[self.blocks(other)], self.landed.at[self.blocks(step)]
        return self.remote(source, target, self.plane_sems, 0, step, device)

    def line_out(self, step):
        other, device = self.ring.in_line(step)
        source, target = self.middle.at[self.pieces(other)], self.lined.at[self.pieces(step)]
        return self.remote(source, target, self.line_sems, 0, step, device)

    def line_back(self, step):
        lines = self.ring.lines
        target = self.whole.at[self.pieces(self.spot * lines + self.ring.at_line)]
        return self.remote(self.total, target, self.line_sems, 1, step, self.ring.in_line(step)[1])

    def plane_back(self, step):
        block = self.whole.at[self.blocks(self.spot)]
        return self.remote(block, block, self.plane_sems, 1, step, self.ring.in_plane(step)[1])

    def across(self, step):
        planes = self.ring.planes
        source = lax.rem(self.ring.at_plane - step + planes, planes)
        block = self.whole.at[self.blocks(self.ring.core * planes + source)]
        return self.remote(block, block, self.plane_sems, 2, step, self.ring.pair)

    def scatter(self):
        self.swap().wait()
        own = self.own[self.halves(self.ring.core), :].astype(jnp.float32)
        self.mine[...] = half(own + self.from_pair[...].astype(jnp.float32))
        for step in range(1, self.ring.planes):
            self.plane_out(step).start()

    def gather_plane(self):
        running = self.mine[self.blocks(self.ring.at_plane), :].astype(jnp.float32)
        for step in range(1, self.ring.planes):
            self.plane_out(step).wait_recv()
            running = running + self.landed[self.blocks(step), :].astype(jnp.float32)
        self.middle[...] = half(running)
        for step in range(1, self.ring.lines):
            self.line_out(step).start()

    def gather_line(self):
        running = self.middle[self.pieces(self.ring.at_line), :].astype(jnp.float32)
        for step in range(1, self.ring.lines):
            self.line_out(step).wait_recv()
            running = running + self.lined[self.pieces(step), :].astype(jnp.float32)
        self.total[...] = half(running)
        for step in range(1, self.ring.lines):
            self.line_back(step).start()
        self.whole[self.pieces(self.spot * self.ring.lines + self.ring.at_line), :] = self.total[...]

    def spread(self):
        for step in range(1, self.ring.lines):
            self.line_back(step).wait_recv()
        for step in range(1, self.ring.planes):
            self.plane_back(step).start()
        self.across(0).start()

    def pass_on(self):
        for step in range(1, self.ring.planes):
            self.plane_back(step).wait_recv()
            self.across(step).start()

    def settle(self):
        for step in range(self.ring.planes):
            self.across(step).wait()
        for step in range(1, self.ring.planes):
            self.plane_out(step).wait_send()
            self.plane_back(step).wait_send()
        for step in range(1, self.ring.lines):
            self.line_out(step).wait_send()
            self.line_back(step).wait_send()


def step_kernel(shapes, slabs, lines, volumes, w1, w2, w3, mg, spread, pick1, pick2, pick3, back2,
                back3, taps, order, out, p1, p2, p3, w1b, w2p, w3p, a2, even3, odd3, even2, odd2,
                rows2, g2, vol, vol_sems, *parts):
    ring = Ring(slabs, lines)
    ring.greet()
    incoming = Exchange(volumes, vol, vol_sems, slabs, ring)
    incoming.start()
    late, early = Summed(ring, *parts[:11]), Summed(ring, *parts[11:])
    late.own[...] = jnp.zeros_like(late.own)
    early.own[...] = jnp.zeros_like(early.own)

    f32 = jnp.float32
    channels = vol.shape[1]
    c1, c2 = w1.shape[0], w2.shape[0]
    blocks = spread.shape[2] // 128
    plane1, plane2 = pick1.shape[0] // 9, pick2.shape[0] // 9
    length2 = mg.shape[0] // plane2
    width1 = blocks * BLOCK * c1
    width2 = length2 * c2

    wide = contract(w1[...], taps[...])
    for pair in range(9):
        tile = wide[:, pair * 128 : (pair + 1) * 128]
        for l in range(BLOCK):
            moved = pltpu.roll(tile, 2 * l * channels, 1) if l else tile
            w1b[l * c1 : (l + 1) * c1, pair * 128 : (pair + 1) * 128] = half(moved)
    w2p[...] = jnp.zeros_like(w2p)
    w3p[...] = jnp.zeros_like(w3p)
    for pair in range(9):
        w2p[:, pair * 128 : pair * 128 + 3 * c1] = w2[:, pair * 3 * c1 : (pair + 1) * 3 * c1]
        w3p[pair * 256 : pair * 256 + 3 * c2, :] = w3[pair * 3 * c2 : (pair + 1) * 3 * c2, :]

    incoming.wait_all()
    levels = []
    for part in range(vol.shape[0]):
        placed = contract(vol[part, 0], spread[0])
        for k in range(1, channels):
            placed = placed + contract(vol[part, k], spread[k])
        levels.append(half(placed))
    r1 = half(contract(pick1[...], jnp.concatenate(levels, axis=0)))
    for pair in range(9):
        for block in range(blocks):
            p1[block * plane1 : (block + 1) * plane1, pair * 128 : (pair + 1) * 128] = r1[
                pair * plane1 : (pair + 1) * plane1, block * 128 : (block + 1) * 128
            ]
    pre1 = contract(p1[...], w1b[...], 1)
    act1 = half(pre1 * sigmoid(pre1))
    a1 = jnp.concatenate(
        [act1[block * plane1 : (block + 1) * plane1, :] for block in range(blocks)], axis=1
    )
    r2 = contract(pick2[...], a1)
    r2 = jnp.concatenate([r2, jnp.zeros((9 * plane2, 128), f32)], axis=1)
    sides = (half(pltpu.roll(r2, c1, 1)), half(pltpu.roll(r2, width1 + 128 - c1, 1)))
    for l in range(length2):
        chunk = sides[l % 2][:, (l // 2) * 128 : (l // 2 + 1) * 128]
        for pair in range(9):
            p2[l * plane2 : (l + 1) * plane2, pair * 128 : (pair + 1) * 128] = chunk[
                pair * plane2 : (pair + 1) * plane2, :
            ]
    pre2 = contract(p2[...], w2p[...], 1)
    act2 = pre2 * sigmoid(pre2)
    for l in range(length2):
        a2[:, l * c2 : (l + 1) * c2] = act2[l * plane2 : (l + 1) * plane2, :]
    r3 = contract(pick3[...], half(a2[...]))
    r3 = jnp.concatenate([r3, jnp.zeros((9 * plane2, 256), f32)], axis=1)
    sides = (half(pltpu.roll(r3, c2, 1)), half(r3))
    for l in range(length2):
        chunk = sides[l % 2][:, (l // 2) * 128 : (l // 2) * 128 + 256]
        for pair in range(9):
            p3[l * plane2 : (l + 1) * plane2, pair * 256 : (pair + 1) * 256] = chunk[
                pair * plane2 : (pair + 1) * plane2, :
            ]
    pre3 = contract(p3[...], w3p[...])
    given = contract(order[...], mg[...])
    slope3 = given * slope_of(pre3)
    delta3 = half(slope3)
    grad3 = contract(half(slope3.T), p3[...])
    for pair in range(9):
        for lane in range(0, 3 * c2, 128):
            wide = min(128, 3 * c2 - lane)
            turned = grad3[:, pair * 256 + lane : pair * 256 + lane + 128].T
            at = pair * 3 * c2 + lane
            late.own[at : at + wide, :] = half(turned[:wide, :])
    late.swap().start()

    spread3 = contract(delta3, w3p[...], 1)
    for pair in range(9):
        for side, holder in ((0, even3), (1, odd3)):
            for tile in range(length2 // 2 + 1):
                total = None
                for part in range(2):
                    l = 2 * (tile - part) + side
                    if 0 <= l < length2:
                        piece = spread3[
                            l * plane2 : (l + 1) * plane2,
                            pair * 256 + part * 128 : pair * 256 + part * 128 + 128,
                        ]
                        total = piece if total is None else total + piece
                holder[pair * plane2 : (pair + 1) * plane2, tile * 128 : (tile + 1) * 128] = total
    down = contract_fine(back3[...], even3[...])
    down = pltpu.roll(down, down.shape[1] - c2, 1) + contract_fine(back3[...], odd3[...])
    for l in range(length2):
        rows2[l * plane2 : (l + 1) * plane2, :] = down[:, l * c2 : (l + 1) * c2]
    slope2 = half(rows2[...]).astype(f32) * slope_of(pre2)
    delta2 = half(slope2)
    late.scatter()
    grad2 = contract(half(slope2.T), p2[...])
    g2[...] = jnp.zeros_like(g2)
    for pair in range(9):
        g2[:, pair * 3 * c1 : (pair + 1) * 3 * c1] = grad2[:, pair * 128 : pair * 128 + 3 * c1]

    spread2 = contract(delta2, w2p[...])
    for pair in range(9):
        for l in range(length2):
            holder = odd2 if l % 2 else even2
            holder[pair * plane2 : (pair + 1) * plane2, (l // 2) * 128 : (l // 2 + 1) * 128] = spread2[
                l * plane2 : (l + 1) * plane2, pair * 128 : (pair + 1) * 128
            ]
    late.gather_plane()
    tail = jnp.zeros((plane1, 128), f32)
    left = jnp.concatenate([contract_fine(back2[...], even2[...]), tail], axis=1)
    right = jnp.concatenate([contract_fine(back2[...], odd2[...]), tail], axis=1)
    down = pltpu.roll(left, width1 + 128 - c1, 1) + pltpu.roll(right, c1, 1)
    step = BLOCK * c1
    down = jnp.concatenate([down[:, block * step : (block + 1) * step] for block in range(blocks)], axis=0)
    slope1 = down * slope_of(pre1)
    grad1 = contract(half(slope1.T), p1[...])
    tiles = []
    for pair in range(9):
        total = grad1[:c1, pair * 128 : (pair + 1) * 128]
        for l in range(1, BLOCK):
            tile = grad1[l * c1 : (l + 1) * c1, pair * 128 : (pair + 1) * 128]
            total = total + pltpu.roll(tile, 128 - 2 * l * channels, 1)
        tiles.append(half(total))
    first = contract(jnp.concatenate(tiles, axis=1), taps[...], 1)

    for index, base, rows, start, width in tiles_of(shapes[:2]):
        if index == 0:
            early.own[base : base + rows, :width] = half(first)
        else:
            early.own[base : base + rows, :] = half(g2[:, start : start + 128])
    early.swap().start()
    late.gather_line()
    early.scatter()
    late.spread()
    early.gather_plane()
    late.pass_on()
    early.gather_line()
    early.spread()
    early.pass_on()
    late.settle()
    early.settle()
    incoming.drain()
    out[: late.whole.shape[0], :] = late.whole[...]
    out[late.whole.shape[0] :, :] = early.whole[...]


def unpack_kernel(shapes, bases, factor, packed, first, second, third):
    for out, shape, base in ((first, shapes[:1], bases[0]), (second, shapes[1:2], bases[1])):
        for index, at, rows, start, width in tiles_of(shape):
            tile = packed[base + at : base + at + rows, :].astype(jnp.float32) * factor
            out[:, start : start + width] = tile[:, :width]
    third[...] = packed[: third.shape[0], :].astype(jnp.float32) * factor


def per_device(volumes, w_first, w_second, w_third, map_grad):
    slabs = lax.axis_size("slab")
    devices = lax.axis_size("vol") * slabs
    chips = devices // 2
    lines = chips // (2 * slabs)
    factor = 1.0 / (map_grad.shape[0] * devices)
    shapes = (w_first.shape, w_second.shape, w_third.shape)
    parts, channels, level, height, width = volumes.shape
    depth = level * slabs
    tables = tables_of(channels, depth, height, width)
    c1, c2, c3 = w_first.shape[0], w_second.shape[0], w_third.shape[0]
    plane1 = depth * height // 4
    plane2 = depth * height // 16
    length2 = width // 4
    cells = plane2 * length2
    bf16, f32 = jnp.bfloat16, jnp.float32
    late_piece = piece_rows(((27 * c2, c3),), devices)
    early_piece = piece_rows(shapes[:2], devices)
    scratch = [
        ((width // (2 * BLOCK) * plane1, 9 * 128), bf16),
        ((cells, 9 * 128), bf16),
        ((cells, 9 * 256), bf16),
        ((BLOCK * c1, 9 * 128), bf16),
        ((c2, 9 * 128), bf16),
        ((9 * 256, c3), bf16),
        ((plane2, length2 * c2), f32),
        ((9 * plane2, length2 * c2 + 128), f32),
        ((9 * plane2, length2 * c2 + 128), f32),
        ((9 * plane2, width // 2 * c1), f32),
        ((9 * plane2, width // 2 * c1), f32),
        ((cells, c2), f32),
        ((c2, pl.cdiv(27 * c1, 128) * 128), f32),
        ((slabs, channels, level * height, width), bf16),
    ]
    scratch = [pltpu.VMEM(shape, kind) for shape, kind in scratch]
    dma = pltpu.SemaphoreType.DMA
    scratch.append(dma((2, slabs)))
    for piece in (late_piece, early_piece):
        for count in (devices, chips, chips, chips, lines, lines, 1, devices):
            scratch.append(pltpu.VMEM((count * piece, 128), bf16))
        scratch += [dma((2,)), dma((3, 2, 2 * slabs)), dma((2, 2, lines))]
    operands = (
        volumes.reshape(parts, channels, level * height, width),
        w_first,
        w_second,
        w_third.T,
        map_grad[0].transpose(1, 2, 3, 0).reshape(cells, c3),
        *tables,
    )
    in_vmem = pl.BlockSpec(memory_space=pltpu.VMEM)
    packed = pl.pallas_call(
        functools.partial(step_kernel, shapes, slabs, lines),
        out_shape=jax.ShapeDtypeStruct((devices * (late_piece + early_piece), 128), bf16),
        in_specs=[in_vmem] * len(operands),
        out_specs=in_vmem,
        scratch_shapes=scratch,
        compiler_params=pltpu.CompilerParams(
            collective_id=0, has_side_effects=True, vmem_limit_bytes=56 << 20
        ),
        name="step",
    )(*operands)
    early_base = devices * late_piece
    bases = (early_base, early_base + packed_rows(shapes[:1]))
    outs = (shapes[0], shapes[1], (27 * c2, c3))
    first, second, third = pl.pallas_call(
        functools.partial(unpack_kernel, shapes, bases, factor),
        out_shape=[jax.ShapeDtypeStruct(shape, f32) for shape in outs],
        in_specs=[in_vmem],
        out_specs=[in_vmem] * 3,
        name="unpack",
    )(packed)
    return first, second, third.T


def solution(mesh):
    return jax.shard_map(
        per_device,
        mesh=mesh,
        in_specs=(
            P("vol", None, "slab", None, None),
            P(),
            P(),
            P(),
            P(("vol", "slab"), None, None, None, None),
        ),
        out_specs=(P(), P(), P()),
        check_vma=False,
    )
```

```python
import functools

import jax
import jax.numpy as jnp
import numpy as np
from jax import lax
from jax.experimental import pallas as pl
from jax.experimental.pallas import tpu as pltpu
from jax.sharding import PartitionSpec as P

MESH = pl.DeviceIdType.MESH
BLOCK = 8


def one_hot(rows, cols, pairs):
    table = np.zeros((rows, cols), np.float32)
    for row, col in pairs:
        table[row, col] = 1.0
    return table


def cell_picks(depth, height, stride):
    out_depth, out_height = depth // stride, height // stride
    pairs = []
    for a in range(3):
        for b in range(3):
            for i in range(out_depth):
                for j in range(out_height):
                    z, y = stride * i + a - 1, stride * j + b - 1
                    if 0 <= z < depth and 0 <= y < height:
                        row = ((a * 3 + b) * out_depth + i) * out_height + j
                        pairs.append((row, z * height + y))
    return one_hot(9 * out_depth * out_height, depth * height, pairs)


def tables_of(channels, depth, height, width):
    blocks = width // (2 * BLOCK)
    spread = np.zeros((channels, width, blocks * 128), np.float32)
    for block in range(blocks):
        for at in range(2 * BLOCK + 1):
            x = 2 * BLOCK * block - 1 + at
            if x >= 0:
                for k in range(channels):
                    spread[k, x, block * 128 + at * channels + k] = 1.0
    taps = one_hot(
        27 * channels,
        9 * 128,
        [
            (pair * 3 * channels + lane, pair * 128 + lane)
            for pair in range(9)
            for lane in range(3 * channels)
        ],
    )
    plane, length = (depth // 4) * (height // 4), width // 4
    order = one_hot(
        plane * length,
        plane * length,
        [(l * plane + p, p * length + l) for l in range(length) for p in range(plane)],
    )
    second = cell_picks(depth // 2, height // 2, 2)
    third = cell_picks(depth // 4, height // 4, 1)
    tables = (spread, cell_picks(depth, height, 2), second, third, second.T, third.T, taps, order)
    return [jnp.asarray(table, jnp.bfloat16) for table in tables]


def contract(lhs, rhs, rhs_dim=0):
    return lax.dot_general(
        lhs, rhs, (((1,), (rhs_dim,)), ((), ())), preferred_element_type=jnp.float32
    )


def contract_fine(lhs, rhs):
    coarse = half(rhs)
    return contract(lhs, coarse) + contract(lhs, half(rhs - coarse.astype(jnp.float32)))


def sigmoid(pre):
    return 1.0 / (1.0 + jnp.exp(-pre))


def slope_of(pre):
    sigma = sigmoid(pre)
    return sigma * (1.0 + pre * (1.0 - sigma))


def half(value):
    return value.astype(jnp.bfloat16)


def packed_rows(shapes):
    return sum(pl.cdiv(cols, 128) * rows for rows, cols in shapes)


def tiles_of(shapes):
    base = 0
    for index, (rows, cols) in enumerate(shapes):
        for start in range(0, cols, 128):
            yield index, base, rows, start, min(128, cols - start)
            base += rows


def piece_rows(shapes, devices):
    return pl.cdiv(pl.cdiv(packed_rows(shapes), devices), 16) * 16


class Exchange:
    def __init__(self, source, held, sems, slabs, ring):
        self.slabs = slabs
        self.source, self.held, self.sems = source, held, sems
        self.vol, self.slab = ring.vol, ring.slab

    def copy(self, step):
        other = lax.rem(self.slab + step, self.slabs)
        return pltpu.make_async_remote_copy(
            src_ref=self.source.at[other],
            dst_ref=self.held.at[self.slab],
            send_sem=self.sems.at[0, step],
            recv_sem=self.sems.at[1, step],
            device_id=(self.vol, other),
            device_id_type=MESH,
        )

    def start(self):
        for step in range(1, self.slabs):
            self.copy(step).start()
        self.held[self.slab] = self.source[self.slab]

    def wait_all(self):
        for step in range(1, self.slabs):
            self.copy(step).wait_recv()

    def drain(self):
        for step in range(1, self.slabs):
            self.copy(step).wait_send()


class Ring:
    def __init__(self, slabs, lines):
        self.slabs, self.lines, self.planes = slabs, lines, 2 * slabs
        self.vol = lax.axis_index("vol")
        self.slab = lax.axis_index("slab")
        self.core = lax.rem(self.vol, 2)
        self.side = lax.rem(self.vol // 2, 2)
        self.at_line = self.vol // 4
        self.at_plane = self.side * slabs + self.slab
        self.pair = (self.vol + 1 - 2 * self.core, self.slab)

    def in_plane(self, step):
        other = lax.rem(self.at_plane + step, self.planes)
        vol = (self.at_line * 2 + other // self.slabs) * 2 + self.core
        return other, (vol, lax.rem(other, self.slabs))

    def in_line(self, step):
        other = lax.rem(self.at_line + step, self.lines)
        return other, ((other * 2 + self.side) * 2 + self.core, self.slab)

    def greet(self):
        barrier = pltpu.get_barrier_semaphore()
        partners = [self.pair]
        partners += [self.in_plane(step)[1] for step in range(1, self.planes)]
        partners += [self.in_line(step)[1] for step in range(1, self.lines)]
        for partner in partners:
            pl.semaphore_signal(barrier, inc=1, device_id=partner, device_id_type=MESH)
        pl.semaphore_wait(barrier, len(partners))


class Summed:
    def __init__(self, ring, own, from_pair, mine, landed, middle, lined, whole, *sems):
        self.ring = ring
        self.own, self.from_pair, self.mine = own, from_pair, mine
        self.landed, self.middle, self.lined = landed, middle, lined
        self.whole = whole
        self.pair_sems, self.plane_sems, self.line_sems = sems
        self.block = middle.shape[0]
        self.half = ring.planes * self.block
        self.spot = ring.core * ring.planes + ring.at_plane

    def blocks(self, index):
        return pl.ds(pl.multiple_of(index * self.block, 16), self.block)

    def halves(self, index):
        return pl.ds(pl.multiple_of(index * self.half, 16), self.half)

    def remote(self, source, target, sems, kind, step, device):
        return pltpu.make_async_remote_copy(
            src_ref=source,
            dst_ref=target,
            send_sem=sems.at[kind, 0, step],
            recv_sem=sems.at[kind, 1, step],
            device_id=device,
            device_id_type=MESH,
        )

    def swap(self):
        return pltpu.make_async_remote_copy(
            src_ref=self.own.at[self.halves(1 - self.ring.core)],
            dst_ref=self.from_pair,
            send_sem=self.pair_sems.at[0],
            recv_sem=self.pair_sems.at[1],
            device_id=self.ring.pair,
            device_id_type=MESH,
        )

    def plane_out(self, step):
        other, device = self.ring.in_plane(step)
        source, target = self.mine.at[self.blocks(other)], self.landed.at[self.blocks(step)]
        return self.remote(source, target, self.plane_sems, 0, step, device)

    def line_out(self, step):
        target = self.lined.at[self.blocks(self.ring.at_line)]
        return self.remote(self.middle, target, self.line_sems, 0, step, self.ring.in_line(step)[1])

    def plane_back(self, step):
        block = self.whole.at[self.blocks(self.spot)]
        return self.remote(block, block, self.plane_sems, 1, step, self.ring.in_plane(step)[1])

    def across(self, step):
        planes = self.ring.planes
        source = lax.rem(self.ring.at_plane - step + planes, planes)
        block = self.whole.at[self.blocks(self.ring.core * planes + source)]
        return self.remote(block, block, self.plane_sems, 2, step, self.ring.pair)

    def scatter(self):
        self.swap().wait()
        own = self.own[self.halves(self.ring.core), :].astype(jnp.float32)
        self.mine[...] = half(own + self.from_pair[...].astype(jnp.float32))
        for step in range(1, self.ring.planes):
            self.plane_out(step).start()

    def gather_plane(self):
        running = self.mine[self.blocks(self.ring.at_plane), :].astype(jnp.float32)
        for step in range(1, self.ring.planes):
            self.plane_out(step).wait_recv()
            running = running + self.landed[self.blocks(step), :].astype(jnp.float32)
        self.middle[...] = half(running)
        for step in range(1, self.ring.lines):
            self.line_out(step).start()

    def gather_line(self):
        self.lined[self.blocks(self.ring.at_line), :] = self.middle[...]
        for step in range(1, self.ring.lines):
            self.line_out(step).wait_recv()
        running = self.lined[: self.block, :].astype(jnp.float32)
        for index in range(1, self.ring.lines):
            running = running + self.lined[self.blocks(index), :].astype(jnp.float32)
        self.whole[self.blocks(self.spot), :] = half(running)

    def spread(self):
        for step in range(1, self.ring.planes):
            self.plane_back(step).start()
        self.across(0).start()

    def pass_on(self):
        for step in range(1, self.ring.planes):
            self.plane_back(step).wait_recv()
            self.across(step).start()

    def settle(self):
        for step in range(self.ring.planes):
            self.across(step).wait()
        for step in range(1, self.ring.planes):
            self.plane_out(step).wait_send()
            self.plane_back(step).wait_send()
        for step in range(1, self.ring.lines):
            self.line_out(step).wait_send()


def step_kernel(shapes, slabs, lines, volumes, w1, w2, w3, mg, spread, pick1, pick2, pick3, back2,
                back3, taps, order, out, p1, p2, p3, w1b, w2p, w3p, a2, even3, odd3, even2, odd2,
                rows2, g2, vol, vol_sems, *parts):
    ring = Ring(slabs, lines)
    ring.greet()
    incoming = Exchange(volumes, vol, vol_sems, slabs, ring)
    incoming.start()
    late, early = Summed(ring, *parts[:10]), Summed(ring, *parts[10:])
    late.own[...] = jnp.zeros_like(late.own)
    early.own[...] = jnp.zeros_like(early.own)

    f32 = jnp.float32
    channels = vol.shape[1]
    c1, c2 = w1.shape[0], w2.shape[0]
    blocks = spread.shape[2] // 128
    plane1, plane2 = pick1.shape[0] // 9, pick2.shape[0] // 9
    length2 = mg.shape[0] // plane2
    width1 = blocks * BLOCK * c1
    width2 = length2 * c2

    wide = contract(w1[...], taps[...])
    for pair in range(9):
        tile = wide[:, pair * 128 : (pair + 1) * 128]
        for l in range(BLOCK):
            moved = pltpu.roll(tile, 2 * l * channels, 1) if l else tile
            w1b[l * c1 : (l + 1) * c1, pair * 128 : (pair + 1) * 128] = half(moved)
    w2p[...] = jnp.zeros_like(w2p)
    w3p[...] = jnp.zeros_like(w3p)
    for pair in range(9):
        w2p[:, pair * 128 : pair * 128 + 3 * c1] = w2[:, pair * 3 * c1 : (pair + 1) * 3 * c1]
        w3p[pair * 256 : pair * 256 + 3 * c2, :] = w3[pair * 3 * c2 : (pair + 1) * 3 * c2, :]

    incoming.wait_all()
    levels = []
    for part in range(vol.shape[0]):
        placed = contract(vol[part, 0], spread[0])
        for k in range(1, channels):
            placed = placed + contract(vol[part, k], spread[k])
        levels.append(half(placed))
    r1 = half(contract(pick1[...], jnp.concatenate(levels, axis=0)))
    for pair in range(9):
        for block in range(blocks):
            p1[block * plane1 : (block + 1) * plane1, pair * 128 : (pair + 1) * 128] = r1[
                pair * plane1 : (pair + 1) * plane1, block * 128 : (block + 1) * 128
            ]
    pre1 = contract(p1[...], w1b[...], 1)
    act1 = half(pre1 * sigmoid(pre1))
    a1 = jnp.concatenate(
        [act1[block * plane1 : (block + 1) * plane1, :] for block in range(blocks)], axis=1
    )
    r2 = contract(pick2[...], a1)
    r2 = jnp.concatenate([r2, jnp.zeros((9 * plane2, 128), f32)], axis=1)
    sides = (half(pltpu.roll(r2, c1, 1)), half(pltpu.roll(r2, width1 + 128 - c1, 1)))
    for l in range(length2):
        chunk = sides[l % 2][:, (l // 2) * 128 : (l // 2 + 1) * 128]
        for pair in range(9):
            p2[l * plane2 : (l + 1) * plane2, pair * 128 : (pair + 1) * 128] = chunk[
                pair * plane2 : (pair + 1) * plane2, :
            ]
    pre2 = contract(p2[...], w2p[...], 1)
    act2 = pre2 * sigmoid(pre2)
    for l in range(length2):
        a2[:, l * c2 : (l + 1) * c2] = act2[l * plane2 : (l + 1) * plane2, :]
    r3 = contract(pick3[...], half(a2[...]))
    r3 = jnp.concatenate([r3, jnp.zeros((9 * plane2, 256), f32)], axis=1)
    sides = (half(pltpu.roll(r3, c2, 1)), half(r3))
    for l in range(length2):
        chunk = sides[l % 2][:, (l // 2) * 128 : (l // 2) * 128 + 256]
        for pair in range(9):
            p3[l * plane2 : (l + 1) * plane2, pair * 256 : (pair + 1) * 256] = chunk[
                pair * plane2 : (pair + 1) * plane2, :
            ]
    pre3 = contract(p3[...], w3p[...])
    given = contract(order[...], mg[...])
    slope3 = given * slope_of(pre3)
    delta3 = half(slope3)
    grad3 = contract(half(slope3.T), p3[...])
    for pair in range(9):
        for lane in range(0, 3 * c2, 128):
            wide = min(128, 3 * c2 - lane)
            turned = grad3[:, pair * 256 + lane : pair * 256 + lane + 128].T
            at = pair * 3 * c2 + lane
            late.own[at : at + wide, :] = half(turned[:wide, :])
    late.swap().start()

    spread3 = contract(delta3, w3p[...], 1)
    for pair in range(9):
        for side, holder in ((0, even3), (1, odd3)):
            for tile in range(length2 // 2 + 1):
                total = None
                for part in range(2):
                    l = 2 * (tile - part) + side
                    if 0 <= l < length2:
                        piece = spread3[
                            l * plane2 : (l + 1) * plane2,
                            pair * 256 + part * 128 : pair * 256 + part * 128 + 128,
                        ]
                        total = piece if total is None else total + piece
                holder[pair * plane2 : (pair + 1) * plane2, tile * 128 : (tile + 1) * 128] = total
    down = contract_fine(back3[...], even3[...])
    down = pltpu.roll(down, down.shape[1] - c2, 1) + contract_fine(back3[...], odd3[...])
    for l in range(length2):
        rows2[l * plane2 : (l + 1) * plane2, :] = down[:, l * c2 : (l + 1) * c2]
    slope2 = half(rows2[...]).astype(f32) * slope_of(pre2)
    delta2 = half(slope2)
    late.scatter()
    grad2 = contract(half(slope2.T), p2[...])
    g2[...] = jnp.zeros_like(g2)
    for pair in range(9):
        g2[:, pair * 3 * c1 : (pair + 1) * 3 * c1] = grad2[:, pair * 128 : pair * 128 + 3 * c1]

    spread2 = contract(delta2, w2p[...])
    for pair in range(9):
        for l in range(length2):
            holder = odd2 if l % 2 else even2
            holder[pair * plane2 : (pair + 1) * plane2, (l // 2) * 128 : (l // 2 + 1) * 128] = spread2[
                l * plane2 : (l + 1) * plane2, pair * 128 : (pair + 1) * 128
            ]
    late.gather_plane()
    tail = jnp.zeros((plane1, 128), f32)
    left = jnp.concatenate([contract_fine(back2[...], even2[...]), tail], axis=1)
    right = jnp.concatenate([contract_fine(back2[...], odd2[...]), tail], axis=1)
    down = pltpu.roll(left, width1 + 128 - c1, 1) + pltpu.roll(right, c1, 1)
    step = BLOCK * c1
    down = jnp.concatenate([down[:, block * step : (block + 1) * step] for block in range(blocks)], axis=0)
    slope1 = down * slope_of(pre1)
    grad1 = contract(half(slope1.T), p1[...])
    tiles = []
    for pair in range(9):
        total = grad1[:c1, pair * 128 : (pair + 1) * 128]
        for l in range(1, BLOCK):
            tile = grad1[l * c1 : (l + 1) * c1, pair * 128 : (pair + 1) * 128]
            total = total + pltpu.roll(tile, 128 - 2 * l * channels, 1)
        tiles.append(half(total))
    first = contract(jnp.concatenate(tiles, axis=1), taps[...], 1)

    for index, base, rows, start, width in tiles_of(shapes[:2]):
        if index == 0:
            early.own[base : base + rows, :width] = half(first)
        else:
            early.own[base : base + rows, :] = half(g2[:, start : start + 128])
    early.swap().start()
    late.gather_line()
    early.scatter()
    late.spread()
    early.gather_plane()
    late.pass_on()
    early.gather_line()
    early.spread()
    early.pass_on()
    late.settle()
    early.settle()
    incoming.drain()
    out[: late.whole.shape[0], :] = late.whole[...]
    out[late.whole.shape[0] :, :] = early.whole[...]


def unpack_kernel(shapes, bases, factor, packed, first, second, third):
    for out, shape, base in ((first, shapes[:1], bases[0]), (second, shapes[1:2], bases[1])):
        for index, at, rows, start, width in tiles_of(shape):
            tile = packed[base + at : base + at + rows, :].astype(jnp.float32) * factor
            out[:, start : start + width] = tile[:, :width]
    third[...] = packed[: third.shape[0], :].astype(jnp.float32) * factor


def per_device(volumes, w_first, w_second, w_third, map_grad):
    slabs = lax.axis_size("slab")
    devices = lax.axis_size("vol") * slabs
    chips = devices // 2
    lines = chips // (2 * slabs)
    factor = 1.0 / (map_grad.shape[0] * devices)
    shapes = (w_first.shape, w_second.shape, w_third.shape)
    parts, channels, level, height, width = volumes.shape
    depth = level * slabs
    tables = tables_of(channels, depth, height, width)
    c1, c2, c3 = w_first.shape[0], w_second.shape[0], w_third.shape[0]
    plane1 = depth * height // 4
    plane2 = depth * height // 16
    length2 = width // 4
    cells = plane2 * length2
    bf16, f32 = jnp.bfloat16, jnp.float32
    late_piece = piece_rows(((27 * c2, c3),), devices)
    early_piece = piece_rows(shapes[:2], devices)
    scratch = [
        ((width // (2 * BLOCK) * plane1, 9 * 128), bf16),
        ((cells, 9 * 128), bf16),
        ((cells, 9 * 256), bf16),
        ((BLOCK * c1, 9 * 128), bf16),
        ((c2, 9 * 128), bf16),
        ((9 * 256, c3), bf16),
        ((plane2, length2 * c2), f32),
        ((9 * plane2, length2 * c2 + 128), f32),
        ((9 * plane2, length2 * c2 + 128), f32),
        ((9 * plane2, width // 2 * c1), f32),
        ((9 * plane2, width // 2 * c1), f32),
        ((cells, c2), f32),
        ((c2, pl.cdiv(27 * c1, 128) * 128), f32),
        ((slabs, channels, level * height, width), bf16),
    ]
    scratch = [pltpu.VMEM(shape, kind) for shape, kind in scratch]
    dma = pltpu.SemaphoreType.DMA
    scratch.append(dma((2, slabs)))
    for piece in (late_piece, early_piece):
        for count in (devices, chips, chips, chips, lines, lines * lines, devices):
            scratch.append(pltpu.VMEM((count * piece, 128), bf16))
        scratch += [dma((2,)), dma((3, 2, 2 * slabs)), dma((1, 2, lines))]
    operands = (
        volumes.reshape(parts, channels, level * height, width),
        w_first,
        w_second,
        w_third.T,
        map_grad[0].transpose(1, 2, 3, 0).reshape(cells, c3),
        *tables,
    )
    in_vmem = pl.BlockSpec(memory_space=pltpu.VMEM)
    packed = pl.pallas_call(
        functools.partial(step_kernel, shapes, slabs, lines),
        out_shape=jax.ShapeDtypeStruct((devices * (late_piece + early_piece), 128), bf16),
        in_specs=[in_vmem] * len(operands),
        out_specs=in_vmem,
        scratch_shapes=scratch,
        compiler_params=pltpu.CompilerParams(
            collective_id=0, has_side_effects=True, vmem_limit_bytes=56 << 20
        ),
        name="step",
    )(*operands)
    early_base = devices * late_piece
    bases = (early_base, early_base + packed_rows(shapes[:1]))
    outs = (shapes[0], shapes[1], (27 * c2, c3))
    first, second, third = pl.pallas_call(
        functools.partial(unpack_kernel, shapes, bases, factor),
        out_shape=[jax.ShapeDtypeStruct(shape, f32) for shape in outs],
        in_specs=[in_vmem],
        out_specs=[in_vmem] * 3,
        name="unpack",
    )(packed)
    return first, second, third.T


def solution(mesh):
    return jax.shard_map(
        per_device,
        mesh=mesh,
        in_specs=(
            P("vol", None, "slab", None, None),
            P(),
            P(),
            P(),
            P(("vol", "slab"), None, None, None, None),
        ),
        out_specs=(P(), P(), P()),
        check_vma=False,
    )
```
